32 devices in a mesh: fsdp: 8 (over z, y), tensor: 4 (over x, core).
Axes of the slice: x: 2, y: 2, z: 4, core: 2. Of those that a mesh axis runs over, the one named last changes fastest.
Arguments:
- images: bfloat16 [2, 8, 577, 1024], P(None, 'fsdp'), may hold values from -6 to 6
- cotangent: bfloat16 [2, 8, 577, 1024], P(None, 'fsdp'), may hold values from -6 to 6
- ln1_gain: bfloat16 [1024], P(('fsdp', 'tensor')), may hold values from 0.5 to 1.5
- ln1_bias: bfloat16 [1024], P(('fsdp', 'tensor')), may hold values from -3 to 3
- qkv_weight: bfloat16 [1024, 16, 192], P('fsdp', 'tensor'), may hold values from -0.1875 to 0.1875
- qv_bias: bfloat16 [16, 128], P('tensor', 'fsdp'), may hold values from -1.1953125 to 1.1953125
- out_weight: bfloat16 [1024, 1024], P('tensor', 'fsdp'), may hold values from -0.75 to 0.75
- out_bias: bfloat16 [1024], P(('fsdp', 'tensor')), may hold values from -3 to 3
- ln2_gain: bfloat16 [1024], P(('fsdp', 'tensor')), may hold values from 0.5 to 1.5
- ln2_bias: bfloat16 [1024], P(('fsdp', 'tensor')), may hold values from -3 to 3
- up_weight: bfloat16 [1024, 4096], P('fsdp', 'tensor'), may hold values from -0.1875 to 0.1875
- up_bias: bfloat16 [4, 1024], P('tensor', 'fsdp'), may hold values from -3 to 3
- down_weight: bfloat16 [4096, 1024], P('tensor', 'fsdp'), may hold values from -0.09375 to 0.09375
- down_bias: bfloat16 [1024], P(('fsdp', 'tensor')), may hold values from -3 to 3
Outputs:
- activations: bfloat16 [2, 8, 577, 1024], P(None, 'fsdp')
- input_grad: float32 [2, 8, 577, 1024], P(None, 'fsdp')
- ln1_gain_grad: float32 [1024], P(('fsdp', 'tensor'))
- ln1_bias_grad: float32 [1024], P(('fsdp', 'tensor'))
- qkv_weight_grad: float32 [1024, 16, 192], P('fsdp', 'tensor')
- qv_bias_grad: float32 [16, 128], P('tensor', 'fsdp')
- out_weight_grad: float32 [1024, 1024], P('tensor', 'fsdp')
- out_bias_grad: float32 [1024], P(('fsdp', 'tensor'))
- ln2_gain_grad: float32 [1024], P(('fsdp', 'tensor'))
- ln2_bias_grad: float32 [1024], P(('fsdp', 'tensor'))
- up_weight_grad: float32 [1024, 4096], P('fsdp', 'tensor')
- up_bias_grad: float32 [4, 1024], P('tensor', 'fsdp')
- down_weight_grad: float32 [4096, 1024], P('tensor', 'fsdp')
- down_bias_grad: float32 [1024], P(('fsdp', 'tensor'))
The draws below stay inside these ranges and needn't reach their ends.
All inputs are finite; a program needn't handle non-finite values.
Results may differ from the reference program's by a relative error of at most 0.023.
Values may be sent and summed in bfloat16 or wider, within the bound.
No kernel may reach another device: no remote copies, remote signals or barrier semaphores. Data moves between devices by JAX's collectives and lax.ppermute only.
A program may use at most 128 MiB of HBM per device.

```python
import jax
import jax.numpy as jnp
from jax import lax

D = 1024
HEADS = 16
HD = 64
FF = 4096
SEQ = 577
MICRO = 2
IMAGES = 8
N_TENSOR = 4


def block_levels(rng, dims, split, low, high):
    factor_of = 1.0
    for position, shards_of in split:
        draws = jax.random.uniform(jax.random.fold_in(jax.random.fold_in(rng, 6), position), (shards_of,), jnp.float32, low / len(split), high / len(split))
        factor_of = factor_of * jnp.repeat(jnp.exp(draws), dims[position] // shards_of).reshape((-1,) + (1,) * (len(dims) - 1 - position))
    return factor_of


def bell_draw(stream_key, extent, width, reach, pieces=(), kind=jnp.bfloat16):
    result = width * jax.random.normal(stream_key, extent, jnp.float32)
    if pieces:
        result = result * block_levels(stream_key, extent, pieces, -0.22, 0.18)
    return jnp.clip(result, -reach, reach).astype(kind)


def setup_inputs(seed: int = 0) -> dict:
    streams_of = jax.random.split(jax.random.key(seed), 15)
    return {
        "images": bell_draw(streams_of[0], (MICRO, IMAGES, SEQ, D), 1.0, 6.0, ((1, 8),)),
        "cotangent": bell_draw(streams_of[1], (MICRO, IMAGES, SEQ, D), 1.0, 6.0, ((1, 8),)),
        "ln1_gain": jnp.clip(0.5 + 1.0 * jax.random.uniform(streams_of[2], (D,), jnp.float32) ** block_levels(streams_of[2], (D,), ((0, 32),), -0.2, 0.2), 0.5, 1.5).astype(jnp.bfloat16),
        "ln1_bias": bell_draw(streams_of[3], (D,), 0.5, 3.0, ((0, 32),)),
        "qkv_weight": bell_draw(streams_of[4], (D, HEADS, 3 * HD), D ** -0.5, 0.1875, ((0, 8), (1, 4))),
        "qv_bias": bell_draw(streams_of[5], (HEADS, 2 * HD), 0.2, 1.1953125, ((0, 4), (1, 8))),
        "out_weight": bell_draw(streams_of[6], (D, D), (D // 16) ** -0.5, 0.75, ((0, 4), (1, 8))),
        "out_bias": bell_draw(streams_of[7], (D,), 0.5, 3.0, ((0, 32),)),
        "ln2_gain": jnp.clip(0.5 + 1.0 * jax.random.uniform(streams_of[8], (D,), jnp.float32) ** block_levels(streams_of[8], (D,), ((0, 32),), -0.2, 0.2), 0.5, 1.5).astype(jnp.bfloat16),
        "ln2_bias": bell_draw(streams_of[9], (D,), 0.5, 3.0, ((0, 32),)),
        "up_weight": bell_draw(streams_of[10], (D, FF), D ** -0.5, 0.1875, ((0, 8), (1, 4))),
        "up_bias": bell_draw(streams_of[11], (N_TENSOR, FF // N_TENSOR), 0.5, 3.0, ((0, 4), (1, 8))),
        "down_weight": bell_draw(streams_of[12], (FF, D), FF ** -0.5, 0.09375, ((0, 4), (1, 8))),
        "down_bias": bell_draw(streams_of[13], (D,), 0.5, 3.0, ((0, 32),)),
    }


@jax.custom_vjp
def low(v):
    return lax.optimization_barrier(v.astype(jnp.bfloat16)).astype(jnp.float32)

@jax.custom_vjp
def low_back(v):
    return v

def low_keep(v):
    return (low(v), None)

def low_pass(kept, grad):
    return (grad,)

def back_keep(v):
    return (v, None)

def back_low(kept, grad):
    return (low(grad),)
low.defvjp(low_keep, low_pass)
low_back.defvjp(back_keep, back_low)
epsilon = 1e-06
highest = lax.Precision.HIGHEST

def layer_norm(values, scale_vec, shift_vec):
    centred = values - lax.optimization_barrier(jnp.mean(values, axis=-1, keepdims=True))
    spread = lax.optimization_barrier(jnp.mean(centred * centred, axis=-1, keepdims=True))
    return centred * lax.rsqrt(spread + epsilon) * scale_vec + shift_vec

def gelu_exact(values):
    return jax.nn.gelu(values, approximate=False)

def forward(picture, ln1_gain, ln1_bias, qkv_weight, qv_bias, out_weight, out_bias, ln2_gain, ln2_bias, up_weight, up_bias, down_weight, down_bias):
    normed_one = low(layer_norm(picture, ln1_gain, ln1_bias))
    projected = jnp.dot(normed_one, qkv_weight.reshape(D, 3 * D), precision=highest).reshape(SEQ, HEADS, 3 * HD)
    queries = low(low_back(projected[:, :, :HD] + qv_bias[:, :HD]))
    key_rows = low(low_back(projected[:, :, HD:2 * HD]))
    val_rows = low(low_back(projected[:, :, 2 * HD:] + qv_bias[:, HD:]))
    scores = low_back(jnp.einsum('shd,thd->hst', queries, key_rows, precision=highest) * HD ** (-0.5))
    weights_low = low(jax.nn.softmax(scores, axis=-1))
    attended = low(low_back(jnp.einsum('hst,thd->shd', weights_low, val_rows, precision=highest).reshape(SEQ, D)))
    branch = low_back(jnp.dot(attended, out_weight, precision=highest) + out_bias)
    hidden_res = picture + branch
    normed_two = low(layer_norm(hidden_res, ln2_gain, ln2_bias))
    pre_act = low_back(jnp.dot(normed_two, up_weight, precision=highest) + up_bias.reshape(FF))
    activated = low(gelu_exact(pre_act))
    mlp_out = low_back(jnp.dot(activated, down_weight, precision=highest) + down_bias)
    return hidden_res + mlp_out

def reference(images, cotangent, ln1_gain, ln1_bias, qkv_weight, qv_bias, out_weight, out_bias, ln2_gain, ln2_bias, up_weight, up_bias, down_weight, down_bias):
    params = (ln1_gain.astype(jnp.float32), ln1_bias.astype(jnp.float32), qkv_weight.astype(jnp.float32), qv_bias.astype(jnp.float32), out_weight.astype(jnp.float32), out_bias.astype(jnp.float32), ln2_gain.astype(jnp.float32), ln2_bias.astype(jnp.float32), up_weight.astype(jnp.float32), up_bias.astype(jnp.float32), down_weight.astype(jnp.float32), down_bias.astype(jnp.float32))
    flat_images = images.reshape(MICRO * IMAGES, SEQ, D).astype(jnp.float32)
    flat_cot = cotangent.reshape(MICRO * IMAGES, SEQ, D).astype(jnp.float32)

    def one_image(running, pair_item):
        picture, cot_image = pair_item
        result_out, pull_back = jax.vjp(forward, picture, *params)
        gradients = pull_back(cot_image)
        updated = tuple((total_old + fresh for total_old, fresh in zip(running, gradients[1:])))
        return (updated, (result_out.astype(jnp.bfloat16), gradients[0]))
    zeroes = tuple((jnp.zeros_like(member) for member in params))
    totals, stacked = lax.scan(one_image, zeroes, (flat_images, flat_cot))
    activations = stacked[0].reshape(images.shape)
    input_grad = stacked[1].reshape(images.shape)
    return (activations, input_grad, totals[0], totals[1], totals[2], totals[3], totals[4], totals[5], totals[6], totals[7], totals[8], totals[9], totals[10], totals[11])
```

```python
import jax
import jax.numpy as jnp
from jax import lax
from jax.experimental import pallas as pl
from jax.experimental.pallas import tpu as pltpu
from jax.sharding import PartitionSpec as P

epsilon = 1e-06
vec_rows = 16
f32 = jnp.float32
bf16 = jnp.bfloat16


def layer_norm(values, scale_vec, shift_vec):
    centred = values - jnp.mean(values, axis=-1, keepdims=True)
    spread = jnp.mean(centred * centred, axis=-1, keepdims=True)
    return centred * lax.rsqrt(spread + epsilon) * scale_vec + shift_vec


def gelu_exact(values):
    return jax.nn.gelu(values, approximate=False)


def matmul(lhs, rhs, dims):
    return lax.dot_general(lhs, rhs, ((dims[0], dims[1]), ((), ())), preferred_element_type=f32)


def swap(value, axis, count, mask):
    return lax.ppermute(value, axis, [(i, i ^ mask) for i in range(count)])


def shift(value, axis, count, by):
    return lax.ppermute(value, axis, [(i, (i + by) % count) for i in range(count)])


def tensor_gather(value):
    count = lax.axis_size("tensor")
    if count != 4:
        return lax.all_gather(value, "tensor", axis=0, tiled=False)
    here = lax.axis_index("tensor")
    result = jnp.zeros((count,) + value.shape, value.dtype)
    for mask in range(count):
        piece = value if mask == 0 else swap(value, "tensor", count, mask)
        result = lax.dynamic_update_index_in_dim(result, piece, here ^ mask, 0)
    return result


def tensor_sum(part):
    count = lax.axis_size("tensor")
    if count != 4:
        return lax.psum(part, "tensor")
    half = part.shape[1] // 2
    even = (lax.axis_index("tensor") & 1) == 0
    low, high = part[:, :half], part[:, half:]
    sent = jnp.where(even, high, low)
    kept = jnp.where(even, low, high)
    got = swap(sent, "tensor", count, 1)
    chip = (kept.astype(f32) + got.astype(f32)).astype(bf16)
    far = swap(chip, "tensor", count, 2)
    total = (chip.astype(f32) + far.astype(f32)).astype(bf16)
    other = swap(total, "tensor", count, 1)
    return jnp.concatenate([jnp.where(even, total, other), jnp.where(even, other, total)], axis=1)


def place_blocks(blocks, owners):
    count = len(blocks)

    def body(owner_ref, *refs):
        for i in range(count):
            refs[count][owner_ref[i]] = refs[i][...]

    return pl.pallas_call(
        body,
        out_shape=jax.ShapeDtypeStruct((count,) + blocks[0].shape, blocks[0].dtype),
        in_specs=[pl.BlockSpec(memory_space=pltpu.SMEM)]
        + [pl.BlockSpec(memory_space=pltpu.VMEM)] * count,
        out_specs=pl.BlockSpec(memory_space=pltpu.VMEM),
        name="place_blocks",
    )(owners, *blocks)


def fsdp_gather(block):
    count = lax.axis_size("fsdp")
    if count != 8:
        return lax.all_gather(block, "fsdp", axis=0, tiled=False)
    here = lax.axis_index("fsdp")
    blocks = [block] + [shift(block, "fsdp", count, 2 * k) for k in (1, 2, 3)]
    owners = [(here - 2 * k) % count for k in range(4)]
    blocks += [swap(member, "fsdp", count, 1) for member in blocks]
    owners += [member ^ 1 for member in owners]
    return place_blocks(blocks, jnp.stack(owners).astype(jnp.int32))


def fsdp_scatter(parts):
    count = lax.axis_size("fsdp")
    if count != 8:
        return lax.psum_scatter(parts, "fsdp", scatter_dimension=0, tiled=False).astype(f32)
    here = lax.axis_index("fsdp")
    line, side = here // 2, here % 2
    pairs = parts.reshape((4, 2) + parts.shape[1:])
    sent = lax.dynamic_index_in_dim(pairs, 1 - side, 1, keepdims=False)
    kept = lax.dynamic_index_in_dim(pairs, side, 1, keepdims=False)
    got = swap(sent, "fsdp", count, 1)
    both = (kept.astype(f32) + got.astype(f32)).astype(bf16)
    total = lax.dynamic_index_in_dim(both, line, 0, keepdims=False).astype(f32)
    for k in (1, 2, 3):
        piece = lax.dynamic_index_in_dim(both, (line + k) % 4, 0, keepdims=False)
        total = total + shift(piece, "fsdp", count, 2 * k).astype(f32)
    return total


def pack_rows(flat, width):
    return jnp.pad(flat, (0, vec_rows * width - flat.shape[0])).reshape(vec_rows, width)


def shards(
    images,
    cotangent,
    ln1_gain,
    ln1_bias,
    qkv_weight,
    qv_bias,
    out_weight,
    out_bias,
    ln2_gain,
    ln2_bias,
    up_weight,
    up_bias,
    down_weight,
    down_bias,
):
    micro_count, images_local, seq_len, model_width = images.shape
    heads = qkv_weight.shape[1]
    head_dim = qkv_weight.shape[2] // 3
    qkv_cols = heads * 3 * head_dim
    att_cols = heads * head_dim
    hidden_local = up_weight.shape[1]
    scale = head_dim ** (-0.5)
    fsdp_count = lax.axis_size("fsdp")
    tensor_count = lax.axis_size("tensor")
    shard_rows = model_width // fsdp_count
    piece_len = ln1_gain.shape[0]

    vectors = jnp.stack([ln1_gain, ln1_bias, out_bias, ln2_gain, ln2_bias, down_bias])
    vectors = tensor_gather(vectors).transpose(1, 0, 2)
    flat = jnp.concatenate([vectors.reshape(-1), qv_bias.reshape(-1), up_bias.reshape(-1)])
    attn_width = qkv_cols + att_cols
    attn_block = jnp.concatenate(
        [
            jnp.concatenate([qkv_weight.reshape(shard_rows, qkv_cols), out_weight.T], axis=1),
            pack_rows(flat, attn_width),
        ],
        axis=0,
    )
    attn_all = fsdp_gather(attn_block)
    up_mat = fsdp_gather(up_weight).reshape(model_width, hidden_local)
    down_t = fsdp_gather(down_weight.T).reshape(model_width, hidden_local)
    qkv_mat = attn_all[:, :shard_rows, :qkv_cols].reshape(model_width, qkv_cols)
    out_t = attn_all[:, :shard_rows, qkv_cols:].reshape(model_width, att_cols)
    rows = attn_all[:, shard_rows:].reshape(fsdp_count, -1)
    n_vec = 6 * shard_rows
    vec6 = rows[:, :n_vec].reshape(fsdp_count, 6, shard_rows).transpose(1, 0, 2)
    vec6 = vec6.reshape(6, model_width).astype(f32)
    gain_one, shift_one, out_shift, gain_two, shift_two, down_shift = [vec6[i] for i in range(6)]
    n_qv = qv_bias.size
    qv_shift = (
        rows[:, n_vec : n_vec + n_qv]
        .reshape(fsdp_count, heads, -1)
        .transpose(1, 0, 2)
        .reshape(heads, 2 * head_dim)
        .astype(f32)
    )
    n_up = up_bias.size
    up_shift = rows[:, n_vec + n_qv : n_vec + n_qv + n_up].reshape(-1).astype(f32)

    items = [(m, i) for m in range(micro_count) for i in range(images_local)]
    state = []
    for m, i in items:
        x_low = images[m, i]
        x = x_low.astype(f32)
        normed, pull_one = jax.vjp(layer_norm, x, gain_one, shift_one)
        act_one = normed.astype(bf16)
        projected = matmul(act_one, qkv_mat, ((1,), (0,))).reshape(seq_len, heads, 3 * head_dim)
        queries = (projected[..., :head_dim] + qv_shift[:, :head_dim]).astype(bf16)
        keys = projected[..., head_dim : 2 * head_dim].astype(bf16)
        vals = (projected[..., 2 * head_dim :] + qv_shift[:, head_dim:]).astype(bf16)
        scores = jnp.einsum("shd,thd->hst", queries, keys, preferred_element_type=f32) * scale
        top = jnp.max(scores, axis=-1, keepdims=True)
        exps = jnp.exp(scores - top)
        denom = jnp.sum(exps, axis=-1, keepdims=True)
        logsum = top + jnp.log(denom)
        low = (exps / denom).astype(bf16)
        attended = jnp.einsum("hst,thd->shd", low, vals, preferred_element_type=f32)
        attended = attended.astype(bf16).reshape(seq_len, att_cols)
        part = matmul(attended, out_t, ((1,), (1,))).astype(bf16)
        state.append([x, pull_one, act_one, queries, keys, vals, logsum, attended, part])
    sums = [tensor_sum(entry[8]) for entry in state]

    d_up = d_down = d_out = d_qkv = 0.0
    d_gain_one = d_shift_one = d_out_shift = d_gain_two = d_shift_two = d_down_shift = 0.0
    d_qv = d_up_shift = 0.0
    second = []
    for (m, i), entry, total in zip(items, state, sums):
        hidden = entry[0] + (total.astype(f32) + out_shift)
        normed, pull_two = jax.vjp(layer_norm, hidden, gain_two, shift_two)
        act_two = normed.astype(bf16)
        pre = matmul(act_two, up_mat, ((1,), (0,))) + up_shift
        gelu, pull_gelu = jax.vjp(gelu_exact, pre)
        activated = gelu.astype(bf16)
        grad_low = cotangent[m, i]
        grad_act = matmul(grad_low, down_t, ((1,), (0,)))
        grad_pre = pull_gelu(grad_act)[0].astype(bf16)
        part_two = matmul(grad_pre, up_mat, ((1,), (1,))).astype(bf16)
        part_out = matmul(activated, down_t, ((1,), (1,))).astype(bf16)
        d_up = d_up + matmul(act_two, grad_pre, ((0,), (0,)))
        d_down = d_down + matmul(grad_low, activated, ((0,), (0,)))
        d_up_shift = d_up_shift + jnp.sum(grad_pre.astype(f32), axis=0)
        d_down_shift = d_down_shift + jnp.sum(grad_low.astype(f32), axis=0)
        second.append((hidden, pull_two, part_two, part_out, grad_low))
    totals_two = [tensor_sum(entry[2]) for entry in second]
    totals_out = [tensor_sum(entry[3]) for entry in second]
    up_own = fsdp_scatter(d_up.astype(bf16).reshape(fsdp_count, shard_rows, hidden_local))
    down_own = fsdp_scatter(d_down.astype(bf16).reshape(fsdp_count, shard_rows, hidden_local)).T

    outputs, third = [], []
    for (m, i), first, entry, total in zip(items, state, second, totals_two):
        _, _, act_one, queries, keys, vals, logsum, attended, _ = first
        grad_norm, step_gain, step_shift = entry[1](total.astype(f32))
        d_gain_two, d_shift_two = d_gain_two + step_gain, d_shift_two + step_shift
        grad_hidden = entry[4].astype(f32) + grad_norm
        grad_branch = grad_hidden.astype(bf16)
        d_out_shift = d_out_shift + jnp.sum(grad_branch.astype(f32), axis=0)
        d_out = d_out + matmul(grad_branch, attended, ((0,), (0,)))
        grad_att = matmul(grad_branch, out_t, ((1,), (0,))).astype(bf16)
        grad_att = grad_att.reshape(seq_len, heads, head_dim)
        scores = jnp.einsum("shd,thd->hst", queries, keys, preferred_element_type=f32) * scale
        probs = jnp.exp(scores - logsum)
        val_grad = jnp.einsum(
            "hst,shd->thd", probs.astype(bf16), grad_att, preferred_element_type=f32
        ).astype(bf16)
        prob_grad = jnp.einsum("shd,thd->hst", grad_att, vals, preferred_element_type=f32)
        inner = jnp.sum(prob_grad * probs, axis=-1, keepdims=True)
        score_grad = (probs * (prob_grad - inner)).astype(bf16)
        query_grad = (
            jnp.einsum("hst,thd->shd", score_grad, keys, preferred_element_type=f32) * scale
        ).astype(bf16)
        key_grad = (
            jnp.einsum("hst,shd->thd", score_grad, queries, preferred_element_type=f32) * scale
        ).astype(bf16)
        d_qv = d_qv + jnp.concatenate(
            [jnp.sum(query_grad.astype(f32), axis=0), jnp.sum(val_grad.astype(f32), axis=0)],
            axis=-1,
        )
        grad_proj = jnp.concatenate([query_grad, key_grad, val_grad], axis=-1)
        grad_proj = grad_proj.reshape(seq_len, qkv_cols)
        d_qkv = d_qkv + matmul(act_one, grad_proj, ((0,), (0,)))
        third.append((grad_hidden, matmul(grad_proj, qkv_mat, ((1,), (1,))).astype(bf16)))
    totals_one = [tensor_sum(entry[1]) for entry in third]
    input_grads = []
    for first, entry, total in zip(state, third, totals_one):
        grad_in, step_gain, step_shift = first[1](total.astype(f32))
        d_gain_one, d_shift_one = d_gain_one + step_gain, d_shift_one + step_shift
        input_grads.append(entry[0] + grad_in)
    for entry, total in zip(second, totals_out):
        outputs.append((entry[0] + (total.astype(f32) + down_shift)).astype(bf16))

    vec_grads = jnp.stack(
        [d_gain_one, d_shift_one, d_out_shift, d_gain_two, d_shift_two, d_down_shift]
    )
    vec_grads = vec_grads.reshape(6, fsdp_count, shard_rows).transpose(1, 0, 2)
    qv_grads = d_qv.reshape(heads, fsdp_count, -1).transpose(1, 0, 2)
    flat = jnp.concatenate(
        [
            vec_grads.reshape(fsdp_count, -1),
            qv_grads.reshape(fsdp_count, -1),
            d_up_shift.reshape(fsdp_count, -1),
        ],
        axis=1,
    ).astype(bf16)
    flat = jnp.pad(flat, ((0, 0), (0, vec_rows * attn_width - flat.shape[1])))
    attn_grads = jnp.concatenate([d_qkv.astype(bf16), d_out.astype(bf16)], axis=1)
    attn_own = fsdp_scatter(
        jnp.concatenate(
            [
                attn_grads.reshape(fsdp_count, shard_rows, attn_width),
                flat.reshape(fsdp_count, vec_rows, attn_width),
            ],
            axis=1,
        )
    )
    qkv_own = attn_own[:shard_rows, :qkv_cols].reshape(shard_rows, heads, 3 * head_dim)
    out_own = attn_own[:shard_rows, qkv_cols:].T
    flat_own = attn_own[shard_rows:].reshape(-1)
    vec_own = flat_own[:n_vec].reshape(6, tensor_count, piece_len)
    vec_own = lax.dynamic_index_in_dim(vec_own, lax.axis_index("tensor"), 1, keepdims=False)
    qv_own = flat_own[n_vec : n_vec + n_qv].reshape(qv_bias.shape)
    up_shift_own = flat_own[n_vec + n_qv : n_vec + n_qv + n_up].reshape(up_bias.shape)
    shape = (micro_count, images_local, seq_len, model_width)
    return (
        jnp.stack(outputs).reshape(shape),
        jnp.stack(input_grads).reshape(shape),
        vec_own[0],
        vec_own[1],
        qkv_own,
        qv_own,
        out_own,
        vec_own[2],
        vec_own[3],
        vec_own[4],
        up_own,
        up_shift_own,
        down_own,
        vec_own[5],
    )


def solution(mesh):
    tokens = P(None, "fsdp", None, None)
    vector = P(("fsdp", "tensor"))
    specs = (
        vector,
        vector,
        P("fsdp", "tensor", None),
        P("tensor", "fsdp"),
        P("tensor", "fsdp"),
        vector,
        vector,
        vector,
        P("fsdp", "tensor"),
        P("tensor", "fsdp"),
        P("tensor", "fsdp"),
        vector,
    )
    return jax.shard_map(
        shards,
        mesh=mesh,
        in_specs=(tokens, tokens) + specs,
        out_specs=(tokens, tokens) + specs,
        check_vma=False,
    )
```
